32 devices in a mesh: ctx: 4 (over y, x), head: 8 (over z, core).
Axes of the slice: x: 2, y: 2, z: 4, core: 2. Of those that a mesh axis runs over, the one named last changes fastest.
Arguments:
- pooled_q: bfloat16 [2, 512, 4096], P(None, 'ctx', 'head'), may hold values from -240 to 240
- pooled_k: bfloat16 [2, 512, 8, 384], P(None, 'ctx'), may hold values from -9.5 to 9.5
- wq: bfloat16 [32, 128, 128], P('head'), may hold values from -0.5 to 0.5
- wk: bfloat16 [8, 384, 128], replicated, may hold values from -0.3125 to 0.3125
- teacher: bfloat16 [2, 32, 512, 512], P(None, 'head', 'ctx'), may hold values from 9.9658966e-05 to 1
- doc_ids: int32 [2, 512], P(None, 'ctx'), may hold values from 0 to 3, never falling along the last dimension, each value on 1 to 256 neighbouring positions
- owner_rows: int32 [512], P('ctx'), may hold values from 0 to 511, as said below
Outputs:
- wq_grad: float32 [32, 128, 128], P('head')
- wk_grad: float32 [3072, 128], P('head')
- row_kl: float32 [2, 32, 512], P(None, 'head', 'ctx')
The draws below stay inside these ranges and needn't reach their ends.
Inputs may be any that keep to these rules, and one draw needn't show every extreme that they name: `owner_rows`: slots of each ctx index hold rising block rows, exactly 128 / 4 of them from each aligned range of 128 rows; every row appears once.
All inputs are finite; a program needn't handle non-finite values.
Results may differ from the reference program's by a relative error of at most 0.0034.
The reference program's roundings to bfloat16 on the way (of `query_gate`, `key_gate`, `diff`, `grad_query` and `grad_key`) count: a program that leaves them out, or rounds other values in their place, can miss the bound.
Values may be sent and summed in bfloat16 or wider, within the bound.
A program may use at most 64 MiB of HBM per device.

```python
import math
import jax
import jax.numpy as jnp
import numpy as np
from jax import lax

H = 32
KVH = 8
DH = 128
GD = 128
SEQS = 2
ROWS_DEV = 128
BLOCKS = 512


def draw_owner_rows(key, part):
    ranges = BLOCKS // ROWS_DEV
    share = ROWS_DEV // ranges
    keys = jax.random.split(jax.random.fold_in(key, 17), ranges)
    perms = jax.vmap(lambda single: jax.random.permutation(single, ROWS_DEV))(keys)
    rows = perms.reshape(ranges, ranges, share) + (jnp.arange(ranges) * ROWS_DEV)[:, None, None]
    rows = jnp.transpose(rows, (1, 0, 2)).reshape(ranges, ROWS_DEV)
    return jnp.sort(rows, axis=1).reshape(BLOCKS).astype(jnp.int32)


def draw_pooled_q(key, part):
    values = jnp.clip(jax.random.normal(jax.random.fold_in(key, 31), (SEQS, BLOCKS, H * DH), jnp.float32), -4.0, 4.0)
    return values.astype(jnp.bfloat16)


def draw_pooled_k(key, part):
    shape_all = (SEQS, BLOCKS, KVH, 3 * DH)
    values = jnp.clip(jax.random.normal(jax.random.fold_in(key, 41), shape_all, jnp.float32), -4.0, 4.0)
    return values.astype(jnp.bfloat16)


def steps_of(key, shape, cuts, least, high):
    factor_of, own = 1.0, jax.random.fold_in(key, 6)
    for dim, blocks in cuts:
        heights = jnp.exp(jax.random.uniform(jax.random.fold_in(own, dim), (blocks,), jnp.float32, least / len(cuts), high / len(cuts)))
        factor_of = factor_of * jnp.repeat(heights, shape[dim] // blocks).reshape([-1 if axis == dim else 1 for axis in range(len(shape))])
    return factor_of


def profile(count, total, bound, slope):
    weights = [(1 << 20) // math.isqrt(rank ** slope) + 1 for rank in range(2, count + 1)]
    spare, given = total - bound - (count - 1), [1] * (count - 1)
    while spare > 0:
        movable = [i for i in range(count - 1) if given[i] < bound]
        whole, budget = sum([weights[i] for i in movable]), spare
        for i in movable:
            extra = min(bound - given[i], max(1, budget * weights[i] // whole), spare)
            given[i] = given[i] + extra
            spare = spare - extra
    return np.array([bound] + given)


def uneven(own_key, number_of, total, limit, skew):
    if number_of == 2:
        one = jax.random.randint(own_key, (), max(1, total - limit), min(limit, total - 1) + 1)
        return jnp.stack([one, total - one])
    tallies = jnp.asarray(profile(number_of, total, limit, skew), jnp.int32)
    couples = (number_of - 1) // 2
    source_of, receiver = tallies[1:1 + 2 * couples:2], tallies[2:2 + 2 * couples:2]
    room = jnp.minimum(source_of - 1, limit - receiver)
    passed = jax.random.randint(jax.random.fold_in(own_key, 1), (couples,), 0, 1 << 20) % (room + 1)
    tallies = tallies.at[1:1 + 2 * couples:2].set(source_of - passed).at[2:2 + 2 * couples:2].set(receiver + passed)
    return tallies[jax.random.permutation(jax.random.fold_in(own_key, 2), number_of)]


def centred(rng, extent, scale, bound, cuts=(), kind=jnp.bfloat16):
    values = jax.random.normal(rng, extent, jnp.float32) * scale
    if len(cuts) > 0:
        values = steps_of(rng, extent, cuts, -0.22, 0.18) * values
    return jnp.clip(values, min=-bound, max=bound).astype(kind)


def setup_inputs(seed: int = 0) -> dict:
    splits = jax.random.split(jax.random.key(seed), 8)
    return {
        "pooled_q": draw_pooled_q(jax.random.fold_in(splits[7], 71), 0),
        "pooled_k": draw_pooled_k(jax.random.fold_in(splits[7], 71), 0),
        "wq": centred(splits[2], (H, DH, GD), DH ** -0.5, 0.5, ((0, 8),)),
        "wk": centred(splits[3], (KVH, 3 * DH, GD), (3 * DH) ** -0.5, 0.3125),
        "teacher": jnp.clip(jnp.exp(math.log(1.0) - 9.213757 * jax.random.uniform(splits[4], (SEQS, H, BLOCKS, BLOCKS), jnp.float32) ** steps_of(splits[4], (SEQS, H, BLOCKS, BLOCKS), ((1, 8), (2, 4)), -0.2, 0.2)), 9.965896606445312e-05, 1.0).astype(jnp.bfloat16),
        "doc_ids": jax.vmap(lambda own: jnp.searchsorted(jnp.cumsum(uneven(own, 4, BLOCKS, BLOCKS // 2, 0)), jnp.arange(BLOCKS), side="right"))(jax.random.split(splits[5], SEQS)).reshape((SEQS, BLOCKS)).astype(jnp.int32),
        "owner_rows": draw_owner_rows(jax.random.fold_in(splits[7], 71), 0),
    }


def one_head(query_rows, key_rows, teacher_rows, allowed):
    scale = 1.0 / math.sqrt(GD)
    raw = scale * jnp.dot(query_rows, key_rows.T, preferred_element_type=jnp.float32)
    top = lax.optimization_barrier(jnp.max(jnp.where(allowed, raw, -1e+30), axis=1, keepdims=True))
    expo = jnp.where(allowed, jnp.exp(jnp.where(allowed, raw - top, 0.0)), 0.0)
    total = lax.optimization_barrier(jnp.sum(expo, axis=1, keepdims=True))
    probs = expo / total
    tch = teacher_rows.astype(jnp.float32)
    mass = lax.optimization_barrier(jnp.sum(jnp.where(allowed, tch, 0.0), axis=1, keepdims=True))
    target = jnp.where(allowed, tch / mass, 0.0)
    log_target = jnp.log(tch) - jnp.log(mass)
    log_probs = raw - top - jnp.log(total)
    kl_rows = lax.optimization_barrier(jnp.sum(jnp.where(allowed, target * (log_target - log_probs), 0.0), axis=1))
    diff = jnp.where(allowed, probs - target, 0.0).astype(jnp.bfloat16)
    grad_query = (scale * jnp.dot(diff, key_rows, preferred_element_type=jnp.float32)).astype(jnp.bfloat16)
    grad_key = (scale * jnp.dot(diff.T, query_rows, preferred_element_type=jnp.float32)).astype(jnp.bfloat16)
    return (kl_rows, grad_query, grad_key)

def reference(pooled_q, pooled_k, wq, wk, teacher, doc_ids, owner_rows):
    group = H // KVH
    queries = pooled_q.reshape(SEQS, BLOCKS, H, DH)
    query_gate = jnp.einsum('sbhd,hde->sbhe', queries.astype(jnp.float32), wq.astype(jnp.float32)).astype(jnp.bfloat16)
    key_gate = jnp.einsum('sbgf,gfe->sbge', pooled_k.astype(jnp.float32), wk.astype(jnp.float32)).astype(jnp.bfloat16)
    kv_of_head = jnp.arange(H) // group
    positions = jnp.arange(BLOCKS)
    wq_grad = jnp.zeros((H, DH, GD), jnp.float32)
    wk_grad = jnp.zeros((KVH, 3 * DH, GD), jnp.float32)
    kl_all = []
    for seq in range(SEQS):
        docs = doc_ids[seq]
        allowed = (positions[None, :] <= positions[:, None]) & (docs[None, :] == docs[:, None])
        q_heads = jnp.transpose(query_gate[seq], (1, 0, 2))
        k_heads = jnp.transpose(key_gate[seq][:, kv_of_head], (1, 0, 2))

        def per_head(items):
            return one_head(items[0], items[1], items[2], allowed)
        kl_rows, grad_query, grad_key = lax.map(per_head, (q_heads, k_heads, teacher[seq]))
        kl_all.append(kl_rows)
        wq_grad = wq_grad + jnp.einsum('bhd,hbe->hde', queries[seq].astype(jnp.float32), grad_query.astype(jnp.float32))
        head_terms = jnp.einsum('hbf,hbe->hfe', jnp.transpose(pooled_k[seq][:, kv_of_head], (1, 0, 2)).astype(jnp.float32), grad_key.astype(jnp.float32))
        wk_grad = wk_grad + lax.optimization_barrier(jnp.sum(head_terms.reshape(KVH, group, 3 * DH, GD), axis=1))
    kl_stack = jnp.stack(kl_all, 0)
    row_kl = jnp.take(kl_stack, owner_rows.astype(jnp.int32), axis=2)
    wk_out = jnp.transpose(wk_grad, (1, 0, 2)).reshape(3 * DH * KVH, GD)
    return (wq_grad, wk_out, row_kl)
```

```python
import functools
import math

import jax
import jax.numpy as jnp
from jax import lax
from jax.experimental import pallas as pl
from jax.experimental.pallas import tpu as pltpu
from jax.sharding import PartitionSpec as P

NEG_FILL = -1e30
MESH = pl.DeviceIdType.MESH
F32 = jnp.float32
BF16 = jnp.bfloat16


def dot_nt(a, b):
    return lax.dot_general(a, b, (((1,), (1,)), ((), ())), preferred_element_type=F32)


def dot_tn(a, b):
    return lax.dot_general(a, b, (((0,), (0,)), ((), ())), preferred_element_type=F32)


def dot_nn(a, b):
    return lax.dot_general(a, b, (((1,), (0,)), ((), ())), preferred_element_type=F32)


def kernel(
    dims,
    pq_hbm, pk_hbm, wq_hbm, wk_hbm, t_hbm, doc_ref, own_ref,
    wq_out, wk_out, kl_out,
    pq, pk, wq, wk, tch, kbuf, qg, qrecv, dsend, drecv, gq, gk,
    wq_part, wq_recv, wq_sum, wq_all, wk_part, wk_recv, wk_sum, wk_all, kl_send, kl_all,
    load_sem, k_send, k_recv, q_send, q_recv, d_send, d_recv, l_send, l_recv,
    a_send, a_recv, b_send, b_recv, e_send, e_recv, f_send, f_recv,
):
    C, D, S, R, L, E, F, KVH, group, W, K, FC = dims
    DH = E if pq.shape[2] == L * E else pq.shape[2] // L
    c = lax.axis_index("ctx")
    d = lax.axis_index("head")
    me = c * D + d
    scale = 1.0 / math.sqrt(E)
    share = group // L

    def remote(src, dst, ssem, rsem, cc, dd):
        return pltpu.make_async_remote_copy(
            src_ref=src, dst_ref=dst, send_sem=ssem, recv_sem=rsem,
            device_id=(cc, dd), device_id_type=MESH,
        )

    barrier = pltpu.get_barrier_semaphore()

    def greet(i, carry):
        @pl.when(i != me)
        def _():
            pl.semaphore_signal(barrier, inc=1, device_id=(i // D, i % D), device_id_type=MESH)
        return carry

    lax.fori_loop(0, C * D, greet, 0)

    g = (d * L) // group
    loads = [
        pltpu.make_async_copy(pk_hbm, pk, load_sem.at[0]),
        pltpu.make_async_copy(wk_hbm.at[g], wk, load_sem.at[1]),
        pltpu.make_async_copy(pq_hbm, pq, load_sem.at[2]),
        pltpu.make_async_copy(wq_hbm, wq, load_sem.at[3]),
    ]
    for k in range(W):
        col = pl.multiple_of(jnp.maximum(c - k, 0) * R, R)
        loads.append(
            pltpu.make_async_copy(t_hbm.at[:, :, :, pl.ds(col, R)], tch.at[k], load_sem.at[4 + k])
        )
    for load in loads:
        load.start()

    loads[0].wait()
    loads[1].wait()
    docs = doc_ref[...].astype(F32)
    for s in range(S):
        kbuf[0, s, 0:R, :] = dot_nn(pk[s], wk[...]).astype(BF16)
        kbuf[0, s, R : R + 16, :] = jnp.broadcast_to(docs[s : s + 1, :], (16, R)).astype(BF16)
    loads[2].wait()
    loads[3].wait()
    for s in range(S):
        for h in range(L):
            qg[s, h] = dot_nn(pq[s, :, h * DH : (h + 1) * DH], wq[h]).astype(BF16)
    for k in range(1, W):
        @pl.when(c < k)
        def _(k=k):
            kbuf[k] = jnp.zeros(kbuf.shape[1:], BF16)

        @pl.when(c + k >= C)
        def _(k=k):
            qrecv[k - 1] = jnp.zeros(qrecv.shape[1:], BF16)
            drecv[k - 1] = jnp.zeros(drecv.shape[1:], BF16)

    pl.semaphore_wait(barrier, C * D - 1)

    def key_copy(k):
        return remote(kbuf.at[0], kbuf.at[k], k_send.at[k - 1], k_recv.at[k - 1], c + k, d)

    def query_copy(k):
        return remote(qg, qrecv.at[k - 1], q_send.at[k - 1], q_recv.at[k - 1], c - k, d)

    def diff_copy(k, s, h):
        return remote(
            dsend.at[k, s, h], drecv.at[k - 1, s, h],
            d_send.at[k - 1, s, h], d_recv.at[k - 1, s, h], c - k, d,
        )

    for k in range(1, W):
        @pl.when(c + k < C)
        def _(k=k):
            key_copy(k).start()
    for k in range(1, W):
        @pl.when(c >= k)
        def _(k=k):
            query_copy(k).start()
    for load in loads[4:]:
        load.wait()
    for k in range(1, W):
        @pl.when(c >= k)
        def _(k=k):
            key_copy(k).wait_recv()

    rows_i = lax.broadcasted_iota(jnp.int32, (R, R), 0)
    cols_i = lax.broadcasted_iota(jnp.int32, (R, R), 1)
    causal = rows_i >= cols_i
    lane = lax.broadcasted_iota(jnp.int32, (R, 128), 1)
    kl_cols = jnp.zeros((R, 128), F32)

    def send_diff(s, h):
        for k in range(1, W):
            @pl.when(c >= k)
            def _(k=k):
                diff_copy(k, s, h).start()

    pending = None
    for s in range(S):
        row_doc = jnp.transpose(jnp.broadcast_to(docs[s : s + 1, :], (R, R)))
        allowed = []
        for k in range(W):
            col_doc = kbuf[k, s, R : R + 16, :].astype(F32)[0:1, :]
            same = row_doc == jnp.broadcast_to(col_doc, (R, R))
            allowed.append(same & (causal if k == 0 else (rows_i >= jnp.where(c >= k, 0, R))))
        for h in range(L):
            q = qg[s, h]
            raws = [dot_nt(q, kbuf[k, s, 0:R, :]) * scale for k in range(W)]
            tops = [jnp.where(allowed[k], raws[k], NEG_FILL) for k in range(W)]
            top = jnp.max(functools.reduce(jnp.maximum, tops), axis=1, keepdims=True)
            expos, tms = [], []
            total = mass = entropy = cross = 0.0
            for k in range(W):
                shifted = jnp.where(allowed[k], raws[k] - top, 0.0)
                expo = jnp.where(allowed[k], jnp.exp(shifted), 0.0)
                t = tch[k, s, h].astype(F32)
                tm = jnp.where(allowed[k], t, 0.0)
                expos.append(expo)
                tms.append(tm)
                total = total + expo
                mass = mass + tm
                entropy = entropy + tm * jnp.log(t)
                cross = cross + tm * shifted
            total = jnp.sum(total, axis=1, keepdims=True)
            mass = jnp.sum(mass, axis=1, keepdims=True)
            inner = jnp.sum(entropy - cross, axis=1, keepdims=True)
            kl = inner / mass - jnp.log(mass) + jnp.log(total)
            kl_cols = jnp.where(lane == s * L + h, kl, kl_cols)
            inv_total = 1.0 / total
            inv_mass = 1.0 / mass
            grad = 0.0
            for k in range(W):
                diff = (expos[k] * inv_total - tms[k] * inv_mass).astype(BF16)
                dsend[k, s, h] = diff
                grad = grad + dot_nn(diff, kbuf[k, s, 0:R, :])
            gq[h, s * R : (s + 1) * R, :] = (scale * grad).astype(BF16)
            if pending is not None:
                send_diff(*pending)
            pending = (s, h)

    kl_send[...] = jnp.transpose(kl_cols)[0 : S * L, :]
    for h in range(L):
        left = jnp.concatenate([pq[s, :, h * DH : (h + 1) * DH] for s in range(S)], axis=0)
        term = dot_tn(left, gq[h])
        step = wq_part.shape[1]
        for i in range(DH // step if step < DH else 1):
            slot = (h * DH) // step + i
            at = (h * DH) % step
            size = min(step, DH)
            wq_part[slot, at : at + size, :] = term[i * size : (i + 1) * size, :]
    send_diff(*pending)

    def others(fn):
        for o in range(1, C):
            fn(o, lax.rem(c + o, C), lax.rem(c + C - o, C))

    def a_copy(o, to):
        return remote(wq_part.at[to], wq_recv.at[o - 1], a_send.at[o - 1], a_recv.at[o - 1], to, d)

    def l_copy(o, to):
        return remote(kl_send, kl_all.at[c], l_send.at[o - 1], l_recv.at[o - 1], to, d)

    def b_copy(o, to):
        return remote(wq_sum, wq_all.at[c], b_send.at[o - 1], b_recv.at[o - 1], to, d)

    def f_copy(o, to):
        return remote(wk_sum, wk_all.at[c], f_send.at[o - 1], f_recv.at[o - 1], to, d)

    others(lambda o, to, fr: a_copy(o, to).start())
    others(lambda o, to, fr: l_copy(o, to).start())

    for k in range(1, W):
        @pl.when(c + k < C)
        def _(k=k):
            remote(
                qg, qrecv.at[k - 1], q_send.at[k - 1], q_recv.at[k - 1], c + k, d
            ).wait_recv()

    for s in range(S):
        for h in range(L):
            total = dot_tn(dsend[0, s, h], qg[s, h])
            for k in range(1, W):
                @pl.when(c + k < C)
                def _(k=k, s=s, h=h):
                    remote(
                        dsend.at[k, s, h], drecv.at[k - 1, s, h],
                        d_send.at[k - 1, s, h], d_recv.at[k - 1, s, h], c + k, d,
                    ).wait_recv()
                total = total + dot_tn(drecv[k - 1, s, h], qrecv[k - 1, s, h])
            gk[s * R : (s + 1) * R, h * E : (h + 1) * E] = (scale * total).astype(BF16)

    left = jnp.concatenate([pk[s] for s in range(S)], axis=0)
    wide = dot_tn(left, gk[...])
    term = wide[:, 0:E]
    for h in range(1, L):
        term = term + wide[:, h * E : (h + 1) * E]
    for i in range(D * K):
        wk_part[i // K, i % K] = term[i * FC : (i + 1) * FC, :]

    own = wq_part[c]
    for o in range(1, C):
        a_copy(o, lax.rem(c + o, C)).wait_recv()
        own = own + wq_recv[o - 1]
    wq_sum[...] = own

    def e_copy(i):
        return remote(
            wk_part.at[i // K % D, i % K], wk_recv.at[c, d],
            e_send.at[i], e_recv.at[c, d], i % K, i // K,
        )

    def scatter(i, carry):
        @pl.when((i % K) * D + i // K != me)
        def _():
            e_copy(i).start()
        return carry

    lax.fori_loop(0, D * K, scatter, 0)
    others(lambda o, to, fr: b_copy(o, to).start())

    wq_all[c] = own

    others(lambda o, to, fr: l_copy(o, fr).wait_recv())
    kl_all[c] = kl_send[...]
    owner = own_ref[...]
    picked = jnp.zeros((S * L, R), F32)
    for cc in range(C):
        hot = (rows_i + cc * R == jnp.broadcast_to(owner, (R, R))).astype(F32)
        picked = picked + lax.dot_general(
            kl_all[cc], hot, (((1,), (0,)), ((), ())),
            precision=lax.Precision.HIGHEST, preferred_element_type=F32,
        )
    for s in range(S):
        kl_out[s] = picked[s * L : (s + 1) * L, :]

    @pl.when(c < K)
    def _():
        wk_recv[c, d] = wk_part[d, c % K]

        def arrive(i, carry):
            cc, dd = i // D, i % D

            @pl.when(i != me)
            def _():
                remote(
                    wk_part.at[0, 0], wk_recv.at[cc, dd],
                    e_send.at[0], e_recv.at[cc, dd], cc, dd,
                ).wait_recv()
            return carry

        lax.fori_loop(0, C * D, arrive, 0)
        for kv in range(KVH):
            acc = None
            for cc in range(C):
                for dd in range(kv * share, (kv + 1) * share):
                    piece = wk_recv[cc, dd]
                    acc = piece if acc is None else acc + piece
            wk_sum[:, kv, :] = acc
        others(lambda o, to, fr: f_copy(o, to).start())
        wk_all[c] = wk_sum[...]

    others(lambda o, to, fr: b_copy(o, to).wait_recv())
    wq_out[...] = wq_all[...]

    for o in range(1, C):
        @pl.when(lax.rem(c + C - o, C) < K)
        def _(o=o):
            f_copy(o, lax.rem(c + o, C)).wait_recv()
    wk_out[...] = wk_all[0:K]

    for k in range(1, W):
        @pl.when(c + k < C)
        def _(k=k):
            key_copy(k).wait_send()

        @pl.when(c >= k)
        def _(k=k):
            query_copy(k).wait_send()
            for s in range(S):
                for h in range(L):
                    diff_copy(k, s, h).wait_send()
    others(lambda o, to, fr: a_copy(o, to).wait_send())
    others(lambda o, to, fr: l_copy(o, to).wait_send())
    others(lambda o, to, fr: b_copy(o, to).wait_send())

    @pl.when(c < K)
    def _():
        others(lambda o, to, fr: f_copy(o, to).wait_send())

    def gone(i, carry):
        @pl.when((i % K) * D + i // K != me)
        def _():
            e_copy(i).wait_send()
        return carry

    lax.fori_loop(0, D * K, gone, 0)


def local(C, D, pooled_q, pooled_k, wq, wk, teacher, doc_ids, owner_rows):
    S, R, width = pooled_q.shape
    L, DH, E = wq.shape
    KVH, F, unused = wk.shape
    group = D * L // KVH
    blocks = teacher.shape[3]
    longest = blocks // 2
    W = min(C, (longest - 2) // R + 2)
    FL = F // D
    K = math.gcd(C, FL)
    FC = FL // K
    CH = L * DH // C
    dims = (C, D, S, R, L, E, F, KVH, group, W, K, FC)
    kv = (lax.axis_index("head") * L) // group
    pk = lax.dynamic_index_in_dim(pooled_k, kv, 2, keepdims=False)
    V = pltpu.VMEM
    dma = pltpu.SemaphoreType.DMA
    any_spec = pl.BlockSpec(memory_space=pl.ANY)
    vmem = pl.BlockSpec(memory_space=pltpu.VMEM)
    n = max(C - 1, 1)
    wq_total, wk_grad, row_kl = pl.pallas_call(
        functools.partial(kernel, dims),
        out_shape=(
            jax.ShapeDtypeStruct((C, CH, E), F32),
            jax.ShapeDtypeStruct((K, FC, KVH, E), F32),
            jax.ShapeDtypeStruct((S, L, R), F32),
        ),
        in_specs=[any_spec] * 5 + [vmem, vmem],
        out_specs=(vmem, vmem, vmem),
        scratch_shapes=[
            V((S, R, width), BF16), V((S, R, F), BF16), V((L, DH, E), BF16), V((F, E), BF16),
            V((W, S, L, R, R), BF16), V((W, S, R + 16, E), BF16), V((S, L, R, E), BF16),
            V((W - 1, S, L, R, E), BF16), V((W, S, L, R, R), BF16), V((W - 1, S, L, R, R), BF16),
            V((L, S * R, E), BF16), V((S * R, L * E), BF16),
            V((C, CH, E), F32), V((n, CH, E), F32), V((CH, E), F32), V((C, CH, E), F32),
            V((D, K, FC, E), F32), V((C, D, FC, E), F32), V((FC, KVH, E), F32),
            V((C, FC, KVH, E), F32), V((S * L, R), F32), V((C, S * L, R), F32),
            dma((4 + W,)), dma((W - 1,)), dma((W - 1,)), dma((W - 1,)), dma((W - 1,)),
            dma((W - 1, S, L)), dma((W - 1, S, L)), dma((n,)), dma((n,)),
            dma((n,)), dma((n,)), dma((n,)), dma((n,)), dma((D * K,)), dma((C, D)),
            dma((n,)), dma((n,)),
        ],
        compiler_params=pltpu.CompilerParams(collective_id=0, has_side_effects=True),
    )(pooled_q, pk, wq, wk, teacher, doc_ids, owner_rows.reshape(1, R))
    return (
        wq_total.reshape(L, DH, E),
        wk_grad.reshape(K * FC * KVH, E),
        row_kl,
    )


def solution(mesh):
    placed = (
        P(None, "ctx", "head"),
        P(None, "ctx", None, None),
        P("head", None, None),
        P(),
        P(None, "head", "ctx", None),
        P(None, "ctx"),
        P("ctx"),
    )
    return jax.shard_map(
        functools.partial(local, mesh.shape["ctx"], mesh.shape["head"]),
        mesh=mesh,
        in_specs=placed,
        out_specs=(P("head", None, None), P("head", None), P(None, "head", "ctx")),
        check_vma=False,
    )
```

```python
import functools
import math

import jax
import jax.numpy as jnp
from jax import lax
from jax.experimental import pallas as pl
from jax.experimental.pallas import tpu as pltpu
from jax.sharding import PartitionSpec as P

NEG_FILL = -1e30
MESH = pl.DeviceIdType.MESH
F32 = jnp.float32
BF16 = jnp.bfloat16


def dot_nt(a, b):
    return lax.dot_general(a, b, (((1,), (1,)), ((), ())), preferred_element_type=F32)


def dot_tn(a, b):
    return lax.dot_general(a, b, (((0,), (0,)), ((), ())), preferred_element_type=F32)


def dot_nn(a, b):
    return lax.dot_general(a, b, (((1,), (0,)), ((), ())), preferred_element_type=F32)


def plan(C, S, W):
    side = math.isqrt(C)
    own = [[j for j in range(C)] for s in range(S)]
    if side * side != C or side != 2:
        return own
    for s in range(0, S, 2):
        own[s][side - 1] = C - 1
    return own


def kernel(
    dims, own,
    pq_hbm, pk_hbm, wq_hbm, wk_hbm, t_hbm, doc_ref, own_ref,
    wq_out, wk_out, kl_out,
    pq, pkall, pkb, wq, wk, tch, kbuf, qbuf, dbuf, gq, gk, acc, term,
    wq_part, wq_recv, wq_sum, wq_all, wk_part, wk_recv, wk_sum, wk_all, kl_send, kl_all,
    load_sem, k_send, k_recv, q_send, q_recv, p_send, p_recv, d_send, d_recv, l_send, l_recv,
    a_send, a_recv, b_send, b_recv, e_send, e_recv, f_send, f_recv,
):
    C, D, S, R, L, E, F, KVH, group, W, K, FC = dims
    DH = wq.shape[1]
    c = lax.axis_index("ctx")
    d = lax.axis_index("head")
    me = c * D + d
    scale = 1.0 / math.sqrt(E)
    share = group // L

    def remote(src, dst, ssem, rsem, cc, dd):
        return pltpu.make_async_remote_copy(
            src_ref=src, dst_ref=dst, send_sem=ssem, recv_sem=rsem,
            device_id=(cc, dd), device_id_type=MESH,
        )

    def pick(values):
        out = jnp.int32(values[0])
        for cc in range(1, C):
            out = jnp.where(c == cc, jnp.int32(values[cc]), out)
        return out

    diff_to = [[[own[s][cc - k] if cc >= k else cc for cc in range(C)] for k in range(W)] for s in range(S)]
    query_to = []
    for s in range(S):
        lists = [sorted({diff_to[s][k][cc] for k in range(W)} - {cc}) for cc in range(C)]
        most = max(len(item) for item in lists)
        query_to.append([[item[t] if t < len(item) else cc for cc, item in enumerate(lists)] for t in range(most)])
    query_from = [
        [[int(any(t[src] == cc for t in query_to[s]) and src != cc) for cc in range(C)] for src in range(C)]
        for s in range(S)
    ]
    owned = []
    for s in range(S):
        lists = [[j for j in range(C) if own[s][j] == cc] for cc in range(C)]
        most = max(len(item) for item in lists)
        owned.append([[item[e] if e < len(item) else -1 for item in lists] for e in range(most)])
    key_to = [[own[s][cc] for cc in range(C)] for s in range(S)]

    barrier = pltpu.get_barrier_semaphore()

    def greet(i, carry):
        @pl.when(i != me)
        def _():
            pl.semaphore_signal(barrier, inc=1, device_id=(i // D, i % D), device_id_type=MESH)
        return carry

    g = (d * L) // group
    loads = [
        pltpu.make_async_copy(pk_hbm, pkall, load_sem.at[0]),
        pltpu.make_async_copy(wk_hbm.at[g], wk, load_sem.at[1]),
        pltpu.make_async_copy(pq_hbm, pq, load_sem.at[2]),
        pltpu.make_async_copy(wq_hbm, wq, load_sem.at[3]),
    ]
    for k in range(W):
        col = pl.multiple_of(jnp.maximum(c - k, 0) * R, R)
        loads.append(
            pltpu.make_async_copy(t_hbm.at[:, :, :, pl.ds(col, R)], tch.at[k], load_sem.at[4 + k])
        )
    for load in loads:
        load.start()
    lax.fori_loop(0, C * D, greet, 0)

    loads[0].wait()
    loads[1].wait()
    docs = doc_ref[...].astype(F32)
    wide_r = lax.broadcasted_iota(jnp.int32, (R, R * KVH), 0)
    wide_c = lax.broadcasted_iota(jnp.int32, (R, R * KVH), 1)
    choose = (wide_c == wide_r * KVH + g).astype(F32).astype(BF16)
    for s in range(S):
        feats = dot_nn(choose, pkall[s]).astype(BF16)
        pkb[c, s] = feats
        kbuf[c, s, 0:R, :] = dot_nn(feats, wk[...]).astype(BF16)
        kbuf[c, s, R : R + 16, :] = jnp.broadcast_to(docs[s : s + 1, :], (16, R)).astype(BF16)
    loads[2].wait()
    loads[3].wait()
    for s in range(S):
        for h in range(L):
            qbuf[c, s, h] = dot_nn(pq[s, :, h * DH : (h + 1) * DH], wq[h]).astype(BF16)

    pl.semaphore_wait(barrier, C * D - 1)

    def key_copy(k, src, to):
        return remote(kbuf.at[src], kbuf.at[src], k_send.at[k - 1], k_recv.at[k - 1], to, d)

    def query_copy(s, t, src, to):
        return remote(qbuf.at[src, s], qbuf.at[src, s], q_send.at[t, s], q_recv.at[src, s], to, d)

    def feat_copy(s, src, to):
        return remote(pkb.at[src, s], pkb.at[src, s], p_send.at[s], p_recv.at[src, s], to, d)

    def diff_copy(k, s, h, src, to):
        return remote(
            dbuf.at[src, s, k, h], dbuf.at[src, s, k, h],
            d_send.at[s, k, h], d_recv.at[src, s, k, h], to, d,
        )

    def each_query(fn):
        for s in range(S):
            for t in range(len(query_to[s])):
                to = pick(query_to[s][t])

                @pl.when(to != c)
                def _(s=s, t=t, to=to):
                    fn(query_copy(s, t, c, to))

    def each_feat(fn):
        for s in range(S):
            if any(key_to[s][cc] != cc for cc in range(C)):
                to = pick(key_to[s])

                @pl.when(to != c)
                def _(s=s, to=to):
                    fn(feat_copy(s, c, to))

    def each_diff(s, h, fn):
        for k in range(W):
            if any(diff_to[s][k][cc] != cc for cc in range(C)):
                to = pick(diff_to[s][k])

                @pl.when(to != c)
                def _(k=k, to=to):
                    fn(diff_copy(k, s, h, c, to))

    for k in range(1, W):
        @pl.when(c + k < C)
        def _(k=k):
            key_copy(k, c, c + k).start()
    each_query(lambda copy: copy.start())
    each_feat(lambda copy: copy.start())
    for load in loads[4:]:
        load.wait()

    rows_i = lax.broadcasted_iota(jnp.int32, (R, R), 0)
    cols_i = lax.broadcasted_iota(jnp.int32, (R, R), 1)
    causal = rows_i >= cols_i
    lane = lax.broadcasted_iota(jnp.int32, (R, 128), 1)
    kl_cols = jnp.zeros((R, 128), F32)
    at = [c] + [jnp.maximum(c - k, 0) for k in range(1, W)]

    for k in range(1, W):
        @pl.when(c >= k)
        def _(k=k):
            key_copy(k, c - k, c).wait_recv()

    pending = None
    for s in range(S):
        row_doc = jnp.transpose(jnp.broadcast_to(docs[s : s + 1, :], (R, R)))
        allowed = []
        for k in range(W):
            col_doc = kbuf[at[k], s, R : R + 16, :].astype(F32)[0:1, :]
            same = row_doc == jnp.broadcast_to(col_doc, (R, R))
            allowed.append(same & (causal if k == 0 else (rows_i >= jnp.where(c >= k, 0, R))))
        for h in range(L):
            q = qbuf[c, s, h]
            raws = [dot_nt(q, kbuf[at[k], s, 0:R, :]) * scale for k in range(W)]
            tops = [jnp.where(allowed[k], raws[k], NEG_FILL) for k in range(W)]
            top = jnp.max(functools.reduce(jnp.maximum, tops), axis=1, keepdims=True)
            expos, tms = [], []
            total = mass = inner = 0.0
            for k in range(W):
                shifted = jnp.where(allowed[k], raws[k] - top, 0.0)
                expo = jnp.where(allowed[k], jnp.exp(shifted), 0.0)
                t = tch[k, s, h].astype(F32)
                tm = jnp.where(allowed[k], t, 0.0)
                expos.append(expo)
                tms.append(tm)
                total = total + expo
                mass = mass + tm
                inner = inner + tm * (jnp.log(t) - shifted)
            total = jnp.sum(total, axis=1, keepdims=True)
            mass = jnp.sum(mass, axis=1, keepdims=True)
            inner = jnp.sum(inner, axis=1, keepdims=True)
            kl = inner / mass - jnp.log(mass) + jnp.log(total)
            kl_cols = jnp.where(lane == s * L + h, kl, kl_cols)
            inv_total = 1.0 / total
            inv_mass = 1.0 / mass
            grad = 0.0
            for k in range(W):
                diff = (expos[k] * inv_total - tms[k] * inv_mass).astype(BF16)
                dbuf[c, s, k, h] = diff
                grad = grad + dot_nn(diff, kbuf[at[k], s, 0:R, :])
            gq[h, s * R : (s + 1) * R, :] = (scale * grad).astype(BF16)
            if pending is not None:
                each_diff(*pending, lambda copy: copy.start())
            pending = (s, h)

    kl_send[...] = jnp.transpose(kl_cols)[0 : S * L, :]
    for h in range(L):
        left = jnp.concatenate([pq[s, :, h * DH : (h + 1) * DH] for s in range(S)], axis=0)
        part = dot_tn(left, gq[h])
        step = wq_part.shape[1]
        size = min(step, DH)
        for i in range(DH // size):
            slot = (h * DH + i * size) // step
            off = (h * DH + i * size) % step
            wq_part[slot, off : off + size, :] = part[i * size : (i + 1) * size, :]
    each_diff(*pending, lambda copy: copy.start())

    def others(fn):
        for o in range(1, C):
            fn(o, lax.rem(c + o, C), lax.rem(c + C - o, C))

    def a_copy(o, to):
        return remote(wq_part.at[to], wq_recv.at[o - 1], a_send.at[o - 1], a_recv.at[o - 1], to, d)

    def l_copy(o, to):
        return remote(kl_send, kl_all.at[c], l_send.at[o - 1], l_recv.at[o - 1], to, d)

    def b_copy(o, to):
        return remote(wq_sum, wq_all.at[c], b_send.at[o - 1], b_recv.at[o - 1], to, d)

    def f_copy(o, to):
        return remote(wk_sum, wk_all.at[c], f_send.at[o - 1], f_recv.at[o - 1], to, d)

    others(lambda o, to, fr: a_copy(o, to).start())
    others(lambda o, to, fr: l_copy(o, to).start())

    for s in range(S):
        for src in range(C):
            if any(query_from[s][src]):
                @pl.when(pick(query_from[s][src]) == 1)
                def _(s=s, src=src):
                    query_copy(s, 0, src, c).wait_recv()

    term[...] = jnp.zeros(term.shape, F32)
    for s in range(S):
        for e in range(len(owned[s])):
            j = pick(owned[s][e])

            @pl.when(j >= 0)
            def _(s=s, e=e, j=j):
                for h in range(L):
                    acc[h] = jnp.zeros((R, E), F32)
                    for k in range(W):
                        src = j + k

                        @pl.when(src < C)
                        def _(h=h, k=k, src=src):
                            @pl.when(src != c)
                            def _():
                                diff_copy(k, s, h, src, c).wait_recv()

                            acc[h] += dot_tn(dbuf[src, s, k, h], qbuf[src, s, h])
                    gk[:, h * E : (h + 1) * E] = (scale * acc[h]).astype(BF16)

                @pl.when(j != c)
                def _():
                    feat_copy(s, j, c).wait_recv()

                wide = dot_tn(pkb[j, s], gk[...])
                part = wide[:, 0:E]
                for h in range(1, L):
                    part = part + wide[:, h * E : (h + 1) * E]
                term[...] += part
    for i in range(D * K):
        wk_part[i // K, i % K] = term[i * FC : (i + 1) * FC, :]

    total = wq_part[c]
    for o in range(1, C):
        a_copy(o, lax.rem(c + o, C)).wait_recv()
        total = total + wq_recv[o - 1]
    wq_sum[...] = total

    def e_copy(i):
        return remote(
            wk_part.at[i // K, i % K], wk_recv.at[c, d],
            e_send.at[i], e_recv.at[c, d], i % K, i // K,
        )

    def scatter(i, carry):
        @pl.when((i % K) * D + i // K != me)
        def _():
            e_copy(i).start()
        return carry

    lax.fori_loop(0, D * K, scatter, 0)
    others(lambda o, to, fr: b_copy(o, to).start())

    wq_all[c] = total

    others(lambda o, to, fr: l_copy(o, fr).wait_recv())
    kl_all[c] = kl_send[...]
    owner = own_ref[...]
    picked = jnp.zeros((S * L, R), F32)
    for cc in range(C):
        hot = (rows_i + cc * R == jnp.broadcast_to(owner, (R, R))).astype(F32)
        picked = picked + lax.dot_general(
            kl_all[cc], hot, (((1,), (0,)), ((), ())),
            precision=lax.Precision.HIGHEST, preferred_element_type=F32,
        )
    for s in range(S):
        kl_out[s] = picked[s * L : (s + 1) * L, :]

    @pl.when(c < K)
    def _():
        wk_recv[c, d] = wk_part[d, c % K]

        def arrive(i, carry):
            cc, dd = i // D, i % D

            @pl.when(i != me)
            def _():
                remote(
                    wk_part.at[0, 0], wk_recv.at[cc, dd],
                    e_send.at[0], e_recv.at[cc, dd], cc, dd,
                ).wait_recv()
            return carry

        lax.fori_loop(0, C * D, arrive, 0)
        for kv in range(KVH):
            part = None
            for cc in range(C):
                for dd in range(kv * share, (kv + 1) * share):
                    piece = wk_recv[cc, dd]
                    part = piece if part is None else part + piece
            wk_sum[:, kv, :] = part
        others(lambda o, to, fr: f_copy(o, to).start())
        wk_all[c] = wk_sum[...]

    others(lambda o, to, fr: b_copy(o, to).wait_recv())
    wq_out[...] = wq_all[...]

    for o in range(1, C):
        @pl.when(lax.rem(c + C - o, C) < K)
        def _(o=o):
            f_copy(o, lax.rem(c + o, C)).wait_recv()
    wk_out[...] = wk_all[0:K]

    for k in range(1, W):
        @pl.when(c + k < C)
        def _(k=k):
            key_copy(k, c, c + k).wait_send()
    each_query(lambda copy: copy.wait_send())
    each_feat(lambda copy: copy.wait_send())
    for s in range(S):
        for h in range(L):
            each_diff(s, h, lambda copy: copy.wait_send())
    others(lambda o, to, fr: a_copy(o, to).wait_send())
    others(lambda o, to, fr: l_copy(o, to).wait_send())
    others(lambda o, to, fr: b_copy(o, to).wait_send())

    @pl.when(c < K)
    def _():
        others(lambda o, to, fr: f_copy(o, to).wait_send())

    def gone(i, carry):
        @pl.when((i % K) * D + i // K != me)
        def _():
            e_copy(i).wait_send()
        return carry

    lax.fori_loop(0, D * K, gone, 0)


def finish(a_ref, b_ref, c_ref, x_ref, y_ref, z_ref):
    x_ref[...] = a_ref[...]
    y_ref[...] = b_ref[...]
    z_ref[...] = c_ref[...]


def local(C, D, pooled_q, pooled_k, wq, wk, teacher, doc_ids, owner_rows):
    S, R, width = pooled_q.shape
    L, DH, E = wq.shape
    KVH, F, unused = wk.shape
    group = D * L // KVH
    blocks = teacher.shape[3]
    longest = blocks // 2
    W = min(C, (longest - 2) // R + 2)
    FL = F // D
    K = math.gcd(C, FL)
    FC = FL // K
    CH = L * DH // C
    dims = (C, D, S, R, L, E, F, KVH, group, W, K, FC)
    V = pltpu.VMEM
    dma = pltpu.SemaphoreType.DMA
    any_spec = pl.BlockSpec(memory_space=pl.ANY)
    vmem = pl.BlockSpec(memory_space=pltpu.VMEM)
    n = max(C - 1, 1)
    outs = (
        jax.ShapeDtypeStruct((C, CH, E), F32),
        jax.ShapeDtypeStruct((K, FC, KVH, E), F32),
        jax.ShapeDtypeStruct((S, L, R), F32),
    )
    results = pl.pallas_call(
        functools.partial(kernel, dims, plan(C, S, W)),
        out_shape=outs,
        in_specs=[any_spec] * 5 + [vmem, vmem],
        out_specs=(vmem, vmem, vmem),
        scratch_shapes=[
            V((S, R, width), BF16), V((S, R * KVH, F), BF16), V((C, S, R, F), BF16),
            V((L, DH, E), BF16), V((F, E), BF16),
            V((W, S, L, R, R), BF16), V((C, S, R + 16, E), BF16), V((C, S, L, R, E), BF16),
            V((C, S, W, L, R, R), BF16),
            V((L, S * R, E), BF16), V((R, L * E), BF16), V((L, R, E), F32), V((F, E), F32),
            V((C, CH, E), F32), V((n, CH, E), F32), V((CH, E), F32), V((C, CH, E), F32),
            V((D, K, FC, E), F32), V((C, D, FC, E), F32), V((FC, KVH, E), F32),
            V((C, FC, KVH, E), F32), V((S * L, R), F32), V((C, S * L, R), F32),
            dma((4 + W,)), dma((W - 1,)), dma((W - 1,)), dma((W, S)), dma((C, S)),
            dma((S,)), dma((C, S)),
            dma((S, W, L)), dma((C, S, W, L)), dma((n,)), dma((n,)),
            dma((n,)), dma((n,)), dma((n,)), dma((n,)), dma((D * K,)), dma((C, D)),
            dma((n,)), dma((n,)),
        ],
        compiler_params=pltpu.CompilerParams(collective_id=0, has_side_effects=True),
    )(
        pooled_q, pooled_k.reshape(S, R * KVH, F), wq, wk, teacher, doc_ids,
        owner_rows.reshape(1, R),
    )
    wq_total, wk_grad, row_kl = pl.pallas_call(
        finish, out_shape=outs, in_specs=[vmem] * 3, out_specs=(vmem,) * 3,
    )(*results)
    return (
        wq_total.reshape(L, DH, E),
        wk_grad.reshape(K * FC * KVH, E),
        row_kl,
    )


def solution(mesh):
    placed = (
        P(None, "ctx", "head"),
        P(None, "ctx", None, None),
        P("head", None, None),
        P(),
        P(None, "head", "ctx", None),
        P(None, "ctx"),
        P("ctx"),
    )
    return jax.shard_map(
        functools.partial(local, mesh.shape["ctx"], mesh.shape["head"]),
        mesh=mesh,
        in_specs=placed,
        out_specs=(P("head", None, None), P("head", None), P(None, "head", "ctx")),
        check_vma=False,
    )
```

```python
import functools
import math

import jax
import jax.numpy as jnp
from jax import lax
from jax.experimental import pallas as pl
from jax.experimental.pallas import tpu as pltpu
from jax.sharding import PartitionSpec as P

NEG_FILL = -1e30
MESH = pl.DeviceIdType.MESH
F32 = jnp.float32
BF16 = jnp.bfloat16


def dot_nt(a, b):
    return lax.dot_general(a, b, (((1,), (1,)), ((), ())), preferred_element_type=F32)


def dot_tn(a, b):
    return lax.dot_general(a, b, (((0,), (0,)), ((), ())), preferred_element_type=F32)


def dot_nn(a, b):
    return lax.dot_general(a, b, (((1,), (0,)), ((), ())), preferred_element_type=F32)


def plan(C, S, W):
    side = math.isqrt(C)
    own = [[j for j in range(C)] for s in range(S)]
    if side * side != C or side != 2:
        return own
    for s in range(0, S, 2):
        own[s][side - 1] = C - 1
    return own


def kernel(
    dims, own,
    pq_hbm, pk_hbm, wq_hbm, wk_hbm, t_hbm, doc_ref, own_ref,
    wq_out, wk_out, kl_out,
    pq, pkall, pkb, wq, wk, tch, kbuf, qbuf, dbuf, gq, gk, acc, term,
    wq_part, wq_recv, wq_sum, wq_all, wk_part, wk_recv, wk_sum, wk_all, kl_send, kl_all,
    load_sem, k_send, k_recv, q_send, q_recv, p_send, p_recv, d_send, d_recv, l_send, l_recv,
    a_send, a_recv, b_send, b_recv, e_send, e_recv, f_send, f_recv,
):
    C, D, S, R, L, E, F, KVH, group, W, K, FC = dims
    DH = wq.shape[1]
    c = lax.axis_index("ctx")
    d = lax.axis_index("head")
    scale = 1.0 / math.sqrt(E)
    share = group // L

    def remote(src, dst, ssem, rsem, cc, dd):
        return pltpu.make_async_remote_copy(
            src_ref=src, dst_ref=dst, send_sem=ssem, recv_sem=rsem,
            device_id=(cc, dd), device_id_type=MESH,
        )

    def pick(values):
        out = jnp.int32(values[0])
        for cc in range(1, C):
            out = jnp.where(c == cc, jnp.int32(values[cc]), out)
        return out

    diff_to = [[[own[s][cc - k] if cc >= k else cc for cc in range(C)] for k in range(W)] for s in range(S)]
    query_to = []
    for s in range(S):
        lists = [sorted({diff_to[s][k][cc] for k in range(W)} - {cc}) for cc in range(C)]
        most = max(len(item) for item in lists)
        query_to.append([[item[t] if t < len(item) else cc for cc, item in enumerate(lists)] for t in range(most)])
    query_from = [
        [[int(any(t[src] == cc for t in query_to[s]) and src != cc) for cc in range(C)] for src in range(C)]
        for s in range(S)
    ]
    owned = []
    for s in range(S):
        lists = [[j for j in range(C) if own[s][j] == cc] for cc in range(C)]
        most = max(len(item) for item in lists)
        owned.append([[item[e] if e < len(item) else -1 for item in lists] for e in range(most)])
    key_to = [[own[s][cc] for cc in range(C)] for s in range(S)]

    barrier = pltpu.get_barrier_semaphore()

    def turn(od):
        return lax.rem(d + od, D)

    def greet(cc, dd):
        pl.semaphore_signal(barrier, inc=1, device_id=(cc, dd), device_id_type=MESH)

    g = (d * L) // group
    loads = [
        pltpu.make_async_copy(pk_hbm, pkall, load_sem.at[0]),
        pltpu.make_async_copy(wk_hbm.at[g], wk, load_sem.at[1]),
        pltpu.make_async_copy(pq_hbm, pq, load_sem.at[2]),
        pltpu.make_async_copy(wq_hbm, wq, load_sem.at[3]),
    ]
    for k in range(W):
        col = pl.multiple_of(jnp.maximum(c - k, 0) * R, R)
        loads.append(
            pltpu.make_async_copy(t_hbm.at[:, :, :, pl.ds(col, R)], tch.at[k], load_sem.at[4 + k])
        )
    for load in loads:
        load.start()
    for od in range(1, D):
        dd = turn(od)
        for cc in range(C):
            greet(cc, dd)
    for o in range(1, C):
        greet(lax.rem(c + o, C), d)

    loads[0].wait()
    loads[1].wait()
    docs = doc_ref[...].astype(F32)
    wide_r = lax.broadcasted_iota(jnp.int32, (R, R * KVH), 0)
    wide_c = lax.broadcasted_iota(jnp.int32, (R, R * KVH), 1)
    choose = (wide_c == wide_r * KVH + g).astype(F32).astype(BF16)
    for s in range(S):
        feats = dot_nn(choose, pkall[s]).astype(BF16)
        pkb[c, s] = feats
        kbuf[c, s, 0:R, :] = dot_nn(feats, wk[...]).astype(BF16)
        kbuf[c, s, R : R + 16, :] = jnp.broadcast_to(docs[s : s + 1, :], (16, R)).astype(BF16)
    loads[2].wait()
    loads[3].wait()
    for s in range(S):
        for h in range(L):
            qbuf[c, s, h] = dot_nn(pq[s, :, h * DH : (h + 1) * DH], wq[h]).astype(BF16)

    pl.semaphore_wait(barrier, C * D - 1)

    def key_copy(k, src, to):
        return remote(kbuf.at[src], kbuf.at[src], k_send.at[k - 1], k_recv.at[k - 1], to, d)

    def query_copy(s, t, src, to):
        return remote(qbuf.at[src, s], qbuf.at[src, s], q_send.at[t, s], q_recv.at[src, s], to, d)

    def feat_copy(s, src, to):
        return remote(pkb.at[src, s], pkb.at[src, s], p_send.at[s], p_recv.at[src, s], to, d)

    def diff_copy(k, s, h, src, to):
        return remote(
            dbuf.at[src, s, k, h], dbuf.at[src, s, k, h],
            d_send.at[s, k, h], d_recv.at[src, s, k, h], to, d,
        )

    def each_query(fn):
        for s in range(S):
            for t in range(len(query_to[s])):
                to = pick(query_to[s][t])

                @pl.when(to != c)
                def _(s=s, t=t, to=to):
                    fn(query_copy(s, t, c, to))

    def each_feat(fn):
        for s in range(S):
            if any(key_to[s][cc] != cc for cc in range(C)):
                to = pick(key_to[s])

                @pl.when(to != c)
                def _(s=s, to=to):
                    fn(feat_copy(s, c, to))

    def each_diff(s, h, fn):
        for k in range(W):
            if any(diff_to[s][k][cc] != cc for cc in range(C)):
                to = pick(diff_to[s][k])

                @pl.when(to != c)
                def _(k=k, to=to):
                    fn(diff_copy(k, s, h, c, to))

    for k in range(1, W):
        @pl.when(c + k < C)
        def _(k=k):
            key_copy(k, c, c + k).start()
    each_query(lambda copy: copy.start())
    each_feat(lambda copy: copy.start())
    for load in loads[4:]:
        load.wait()

    rows_i = lax.broadcasted_iota(jnp.int32, (R, R), 0)
    cols_i = lax.broadcasted_iota(jnp.int32, (R, R), 1)
    causal = rows_i >= cols_i
    lane = lax.broadcasted_iota(jnp.int32, (R, 128), 1)
    kl_cols = jnp.zeros((R, 128), F32)
    at = [c] + [jnp.maximum(c - k, 0) for k in range(1, W)]

    for k in range(1, W):
        @pl.when(c >= k)
        def _(k=k):
            key_copy(k, c - k, c).wait_recv()

    pending = []
    for s in range(S):
        row_doc = jnp.transpose(jnp.broadcast_to(docs[s : s + 1, :], (R, R)))
        allowed = []
        for k in range(W):
            col_doc = kbuf[at[k], s, R : R + 16, :].astype(F32)[0:1, :]
            same = row_doc == jnp.broadcast_to(col_doc, (R, R))
            allowed.append(same & (causal if k == 0 else (rows_i >= jnp.where(c >= k, 0, R))))
        for h in range(L):
            q = qbuf[c, s, h]
            raws = [dot_nt(q, kbuf[at[k], s, 0:R, :]) * scale for k in range(W)]
            tops = [jnp.where(allowed[k], raws[k], NEG_FILL) for k in range(W)]
            top = jnp.max(functools.reduce(jnp.maximum, tops), axis=1, keepdims=True)
            expos, tms = [], []
            total = mass = inner = 0.0
            for k in range(W):
                shifted = jnp.where(allowed[k], raws[k] - top, 0.0)
                expo = jnp.where(allowed[k], jnp.exp(shifted), 0.0)
                t = tch[k, s, h].astype(F32)
                tm = jnp.where(allowed[k], t, 0.0)
                expos.append(expo)
                tms.append(tm)
                total = total + expo
                mass = mass + tm
                inner = inner + tm * (jnp.log(t) - shifted)
            total = jnp.sum(total, axis=1, keepdims=True)
            mass = jnp.sum(mass, axis=1, keepdims=True)
            inner = jnp.sum(inner, axis=1, keepdims=True)
            kl = inner / mass - jnp.log(mass) + jnp.log(total)
            kl_cols = jnp.where(lane == s * L + h, kl, kl_cols)
            inv_total = 1.0 / total
            inv_mass = 1.0 / mass
            grad = 0.0
            for k in range(W):
                diff = (expos[k] * inv_total - tms[k] * inv_mass).astype(BF16)
                dbuf[c, s, k, h] = diff
                grad = grad + dot_nn(diff, kbuf[at[k], s, 0:R, :])
            gq[h, s * R : (s + 1) * R, :] = (scale * grad).astype(BF16)
            pending.append((s, h))
            if len(pending) == 2:
                each_diff(*pending.pop(0), lambda copy: copy.start())

    kl_send[...] = jnp.transpose(kl_cols)[0 : S * L, :]
    for h in range(L):
        left = jnp.concatenate([pq[s, :, h * DH : (h + 1) * DH] for s in range(S)], axis=0)
        part = dot_tn(left, gq[h])
        step = wq_part.shape[1]
        size = min(step, DH)
        for i in range(DH // size):
            slot = (h * DH + i * size) // step
            off = (h * DH + i * size) % step
            wq_part[slot, off : off + size, :] = part[i * size : (i + 1) * size, :]
    for item in pending:
        each_diff(*item, lambda copy: copy.start())

    def others(fn):
        for o in range(1, C):
            fn(o, lax.rem(c + o, C), lax.rem(c + C - o, C))

    def a_copy(o, to):
        return remote(wq_part.at[to], wq_recv.at[o - 1], a_send.at[o - 1], a_recv.at[o - 1], to, d)

    def l_copy(o, to):
        return remote(kl_send, kl_all.at[c], l_send.at[o - 1], l_recv.at[o - 1], to, d)

    def b_copy(o, to):
        return remote(wq_sum, wq_all.at[c], b_send.at[o - 1], b_recv.at[o - 1], to, d)

    def f_copy(o, to):
        return remote(wk_sum, wk_all.at[c], f_send.at[o - 1], f_recv.at[o - 1], to, d)

    others(lambda o, to, fr: a_copy(o, to).start())
    others(lambda o, to, fr: l_copy(o, to).start())

    for s in range(S):
        for src in range(C):
            if any(query_from[s][src]):
                @pl.when(pick(query_from[s][src]) == 1)
                def _(s=s, src=src):
                    query_copy(s, 0, src, c).wait_recv()

    term[...] = jnp.zeros(term.shape, F32)
    for s in range(S):
        for e in range(len(owned[s])):
            j = pick(owned[s][e])

            @pl.when(j >= 0)
            def _(s=s, e=e, j=j):
                for k in range(W):
                    src = j + k

                    @pl.when((src < C) & (src != c))
                    def _(k=k, src=src):
                        for h in range(L):
                            diff_copy(k, s, h, src, c).wait_recv()

                    def product(h, k=k, src=src):
                        return dot_tn(dbuf[src, s, k, h], qbuf[src, s, h])

                    if k == 0:
                        for h in range(L):
                            acc[h] = product(h)
                    else:
                        @pl.when(src < C)
                        def _(product=product):
                            for h in range(L):
                                acc[h] += product(h)
                for h in range(L):
                    gk[:, h * E : (h + 1) * E] = (scale * acc[h]).astype(BF16)

                @pl.when(j != c)
                def _():
                    feat_copy(s, j, c).wait_recv()

                wide = dot_tn(pkb[j, s], gk[...])
                part = wide[:, 0:E]
                for h in range(1, L):
                    part = part + wide[:, h * E : (h + 1) * E]
                term[...] += part
    for i in range(D * K):
        wk_part[i // K, i % K] = term[i * FC : (i + 1) * FC, :]

    def e_copy(od, kk):
        dd = turn(od)
        return remote(
            wk_part.at[dd, kk], wk_recv.at[c, d],
            e_send.at[od * K + kk], e_recv.at[c, d], kk, dd,
        )

    def each_part(fn):
        for od in range(1, D):
            for kk in range(K):
                fn(e_copy(od, kk))
        for kk in range(K):
            @pl.when(kk != c)
            def _(kk=kk):
                fn(e_copy(0, kk))

    each_part(lambda copy: copy.start())

    total = wq_part[c]
    for o in range(1, C):
        a_copy(o, lax.rem(c + o, C)).wait_recv()
        total = total + wq_recv[o - 1]
    wq_sum[...] = total


    wq_all[c] = total

    others(lambda o, to, fr: l_copy(o, fr).wait_recv())
    kl_all[c] = kl_send[...]
    owner = own_ref[...]
    picked = jnp.zeros((S * L, R), F32)
    for cc in range(C):
        hot = (rows_i + cc * R == jnp.broadcast_to(owner, (R, R))).astype(F32)
        picked = picked + lax.dot_general(
            kl_all[cc], hot, (((1,), (0,)), ((), ())),
            precision=lax.Precision.HIGHEST, preferred_element_type=F32,
        )
    for s in range(S):
        kl_out[s] = picked[s * L : (s + 1) * L, :]
    others(lambda o, to, fr: b_copy(o, to).start())

    @pl.when(c < K)
    def _():
        wk_recv[c, d] = wk_part[d, c % K]

        def came_copy(cc, dd):
            return remote(wk_part.at[0, 0], wk_recv.at[cc, dd], e_send.at[0], e_recv.at[cc, dd], cc, dd)

        for o in range(1, C):
            came_copy(lax.rem(c + o, C), d).wait_recv()
        for od in range(1, D):
            dd = turn(od)
            for cc in range(C):
                came_copy(cc, dd).wait_recv()
        for kv in range(KVH):
            part = None
            for cc in range(C):
                for dd in range(kv * share, (kv + 1) * share):
                    piece = wk_recv[cc, dd]
                    part = piece if part is None else part + piece
            wk_sum[:, kv, :] = part
        others(lambda o, to, fr: f_copy(o, to).start())
        wk_all[c] = wk_sum[...]

    others(lambda o, to, fr: b_copy(o, to).wait_recv())
    wq_out[...] = wq_all[...]

    for o in range(1, C):
        @pl.when(lax.rem(c + C - o, C) < K)
        def _(o=o):
            f_copy(o, lax.rem(c + o, C)).wait_recv()
    wk_out[...] = wk_all[0:K]

    for k in range(1, W):
        @pl.when(c + k < C)
        def _(k=k):
            key_copy(k, c, c + k).wait_send()
    each_query(lambda copy: copy.wait_send())
    each_feat(lambda copy: copy.wait_send())
    for s in range(S):
        for h in range(L):
            each_diff(s, h, lambda copy: copy.wait_send())
    others(lambda o, to, fr: a_copy(o, to).wait_send())
    others(lambda o, to, fr: l_copy(o, to).wait_send())
    others(lambda o, to, fr: b_copy(o, to).wait_send())

    @pl.when(c < K)
    def _():
        others(lambda o, to, fr: f_copy(o, to).wait_send())

    each_part(lambda copy: copy.wait_send())


def finish(a_ref, b_ref, c_ref, x_ref, y_ref, z_ref):
    x_ref[...] = a_ref[...]
    y_ref[...] = b_ref[...]
    z_ref[...] = c_ref[...]


def local(C, D, pooled_q, pooled_k, wq, wk, teacher, doc_ids, owner_rows):
    S, R, width = pooled_q.shape
    L, DH, E = wq.shape
    KVH, F, unused = wk.shape
    group = D * L // KVH
    blocks = teacher.shape[3]
    longest = blocks // 2
    W = min(C, (longest - 2) // R + 2)
    FL = F // D
    K = math.gcd(C, FL)
    FC = FL // K
    CH = L * DH // C
    dims = (C, D, S, R, L, E, F, KVH, group, W, K, FC)
    V = pltpu.VMEM
    dma = pltpu.SemaphoreType.DMA
    any_spec = pl.BlockSpec(memory_space=pl.ANY)
    vmem = pl.BlockSpec(memory_space=pltpu.VMEM)
    n = max(C - 1, 1)
    outs = (
        jax.ShapeDtypeStruct((C, CH, E), F32),
        jax.ShapeDtypeStruct((K, FC, KVH, E), F32),
        jax.ShapeDtypeStruct((S, L, R), F32),
    )
    results = pl.pallas_call(
        functools.partial(kernel, dims, plan(C, S, W)),
        out_shape=outs,
        in_specs=[any_spec] * 5 + [vmem, vmem],
        out_specs=(vmem, vmem, vmem),
        scratch_shapes=[
            V((S, R, width), BF16), V((S, R * KVH, F), BF16), V((C, S, R, F), BF16),
            V((L, DH, E), BF16), V((F, E), BF16),
            V((W, S, L, R, R), BF16), V((C, S, R + 16, E), BF16), V((C, S, L, R, E), BF16),
            V((C, S, W, L, R, R), BF16),
            V((L, S * R, E), BF16), V((R, L * E), BF16), V((L, R, E), F32), V((F, E), F32),
            V((C, CH, E), F32), V((n, CH, E), F32), V((CH, E), F32), V((C, CH, E), F32),
            V((D, K, FC, E), F32), V((C, D, FC, E), F32), V((FC, KVH, E), F32),
            V((C, FC, KVH, E), F32), V((S * L, R), F32), V((C, S * L, R), F32),
            dma((4 + W,)), dma((W - 1,)), dma((W - 1,)), dma((W, S)), dma((C, S)),
            dma((S,)), dma((C, S)),
            dma((S, W, L)), dma((C, S, W, L)), dma((n,)), dma((n,)),
            dma((n,)), dma((n,)), dma((n,)), dma((n,)), dma((D * K,)), dma((C, D)),
            dma((n,)), dma((n,)),
        ],
        compiler_params=pltpu.CompilerParams(collective_id=0, has_side_effects=True),
    )(
        pooled_q, pooled_k.reshape(S, R * KVH, F), wq, wk, teacher, doc_ids,
        owner_rows.reshape(1, R),
    )
    wq_total, wk_grad, row_kl = pl.pallas_call(
        finish, out_shape=outs, in_specs=[vmem] * 3, out_specs=(vmem,) * 3,
    )(*results)
    return (
        wq_total.reshape(L, DH, E),
        wk_grad.reshape(K * FC * KVH, E),
        row_kl,
    )


def solution(mesh):
    placed = (
        P(None, "ctx", "head"),
        P(None, "ctx", None, None),
        P("head", None, None),
        P(),
        P(None, "head", "ctx", None),
        P(None, "ctx"),
        P("ctx"),
    )
    return jax.shard_map(
        functools.partial(local, mesh.shape["ctx"], mesh.shape["head"]),
        mesh=mesh,
        in_specs=placed,
        out_specs=(P("head", None, None), P("head", None), P(None, "head", "ctx")),
        check_vma=False,
    )
```
